1024 devices in a mesh: wide: 32 (over z, y_lo), narrow: 32 (over y_hi, x, core).
Axes of the slice: x: 8, y: 8 (y_hi: 2, y_lo: 4; y = y_hi * 4 + y_lo), z: 8, core: 2. Of those that a mesh axis runs over, the one named last changes fastest.
Arguments:
- tokens: bfloat16 [131072, 4096], P(('wide', 'narrow')), may hold values from -24 to 24
- norm_gain: bfloat16 [4096], P('narrow'), may hold values from 0.099609375 to 1.8984375
- key_weight: bfloat16 [4096, 512], P('narrow'), may hold values from -0.09375 to 0.09375
- key_grad: bfloat16 [131072, 512], P(('wide', 'narrow')), may hold values from -6 to 6
Outputs:
- keys: bfloat16 [131072, 512], P(('wide', 'narrow'))
- weight_grad: float32 [4096, 512], P('narrow')
- gain_grad: float32 [4096], P('narrow')
The draws below stay inside these ranges and needn't reach their ends.
All inputs are finite; a program needn't handle non-finite values.
Results may differ from the reference program's by a relative error of at most 0.0057.
Values may be sent and summed in bfloat16 or wider, within the bound.
A program may use at most 32 MiB of HBM per device.

```python
import math
import jax
import jax.numpy as jnp
from jax import lax

D = 4096
KH = 4
HD = 128
KV = 512
TOK_DEV = 128
SEQ = 4096
TOKENS = 131072


def with_spikes(entries, own_key, source, target, shards_of, factor):
    def block_of(dim):
        return (jnp.arange(entries.shape[dim]) // (entries.shape[dim] // shards_of)).reshape((-1,) + (1,) * (entries.ndim - 1 - dim))

    first = jax.random.permutation(own_key, shards_of)[block_of(target)]
    far = (block_of(target) + shards_of // 2) % shards_of
    return jnp.where((block_of(source) == first) | (block_of(source) == far), factor * entries, entries)


def steps_of(stream_key, dims, pieces, smallest, largest):
    def one(axis_at, blocks):
        steps = jax.random.uniform(jax.random.fold_in(jax.random.fold_in(stream_key, 6), axis_at), (blocks,), jnp.float32, smallest / len(pieces), largest / len(pieces))
        return jnp.repeat(jnp.exp(steps), dims[axis_at] // blocks).reshape((-1,) + (1,) * (len(dims) - axis_at - 1))

    level = one(*pieces[0])
    for cut in pieces[1:]:
        level = level * one(*cut)
    return level


def centred(stream_key, dims, deviation, reach, split=(), held_as=jnp.bfloat16):
    loudness = steps_of(stream_key, dims, split, -0.22, 0.18) if split else 1.0
    values = jax.random.normal(stream_key, dims, jnp.float32) * deviation * loudness
    return jnp.minimum(jnp.maximum(values, -reach), reach).astype(held_as)


def bell_draw_with(own_key, extent, scale, bound, split, heavy, kind=jnp.bfloat16):
    array = scale * jax.random.normal(own_key, extent, jnp.float32)
    if split:
        array = array * steps_of(own_key, extent, split, -0.22, 0.18)
    return jnp.clip(with_spikes(array, jax.random.fold_in(own_key, 3), *heavy), -bound, bound).astype(kind)


def setup_inputs(seed: int = 0) -> dict:
    seeds = jax.random.split(jax.random.key(seed), 5)
    tokens = bell_draw_with(seeds[0], (TOKENS, D), 1.0, 24.0, ((0, 1024),), (0, 1, 1024, 6.0))
    norm_gain = jnp.clip(1.0 + 0.18 * jax.random.normal(seeds[1], (D,), jnp.float32), 0.099609375, 1.8984375).astype(jnp.bfloat16)
    key_weight = centred(seeds[2], (D, KV), D ** -0.5, 0.09375, ((0, 32),))
    key_grad = centred(seeds[3], (TOKENS, KV), 1.0, 6.0, ((0, 1024),))
    return {"tokens": tokens, "norm_gain": norm_gain, "key_weight": key_weight, "key_grad": key_grad}


rope_base = 500000.0
norm_eps = 1e-05

def rope_tables(first_row, row_count, head_size):
    position = ((first_row + jnp.arange(row_count, dtype=jnp.int32)) % SEQ).astype(jnp.float32)
    halves = jnp.arange(head_size // 2, dtype=jnp.float32)
    frequency = rope_base ** (-2.0 * halves / head_size)
    angle = position[:, None] * frequency[None, :]
    return (jnp.cos(angle), jnp.sin(angle))

def rotate_keys(projected, cosine, sine_table):
    rows = projected.shape[0]
    heads = projected.reshape(rows, KH, HD)
    front_half = heads[:, :, :HD // 2]
    back_half = heads[:, :, HD // 2:]
    cosine = cosine[:, None, :]
    sine_table = sine_table[:, None, :]
    joined = jnp.concatenate([front_half * cosine - back_half * sine_table, back_half * cosine + front_half * sine_table], axis=2)
    return joined.reshape(rows, KV)

def rotate_back(upstream, cosine, sine_table):
    rows = upstream.shape[0]
    heads = upstream.reshape(rows, KH, HD)
    grad_front = heads[:, :, :HD // 2]
    grad_back = heads[:, :, HD // 2:]
    cosine = cosine[:, None, :]
    sine_table = sine_table[:, None, :]
    joined = jnp.concatenate([grad_front * cosine + grad_back * sine_table, grad_back * cosine - grad_front * sine_table], axis=2)
    return joined.reshape(rows, KV)

def layer_block(tokens, norm_gain, key_weight, key_grad, first_row, grad_scale):
    widened = tokens.astype(jnp.float32)
    inv_rms = lax.rsqrt(lax.optimization_barrier(jnp.mean(widened * widened, axis=1, keepdims=True)) + norm_eps)
    normed = widened * inv_rms
    hidden_in = (normed * norm_gain.astype(jnp.float32)[None, :]).astype(jnp.bfloat16)
    projected = jnp.dot(hidden_in, key_weight, preferred_element_type=jnp.float32)
    cosine, sine_table = rope_tables(first_row, tokens.shape[0], HD)
    keys = rotate_keys(projected, cosine, sine_table).astype(jnp.bfloat16)
    pre_grad = rotate_back(key_grad.astype(jnp.float32), cosine, sine_table).astype(jnp.bfloat16)
    weight_term = lax.dot_general(hidden_in, pre_grad, (((0,), (0,)), ((), ())), preferred_element_type=jnp.float32) * grad_scale
    hidden_grad = lax.dot_general(pre_grad, key_weight, (((1,), (1,)), ((), ())), preferred_element_type=jnp.float32)
    gain_part = lax.optimization_barrier(jnp.sum(hidden_grad * normed, axis=0)) * grad_scale
    weight_part = lax.optimization_barrier(weight_term.astype(jnp.bfloat16)).astype(jnp.float32)
    return (keys, weight_part, gain_part)

def reference(tokens, norm_gain, key_weight, key_grad):
    block_rows = TOK_DEV
    block_count = TOKENS // block_rows
    grad_scale = 1.0 / math.sqrt(TOKENS)
    token_blocks = tokens.reshape(block_count, block_rows, D)
    grad_blocks = key_grad.reshape(block_count, block_rows, KV)

    def accumulate(running, inputs):
        weight_sum, gain_sum = running
        block_index, token_block, grad_block = inputs
        keys, weight_part, gain_part = layer_block(token_block, norm_gain, key_weight, grad_block, block_index * block_rows, grad_scale)
        return ((weight_sum + weight_part, gain_sum + gain_part), keys)
    initial = (jnp.zeros((D, KV), jnp.float32), jnp.zeros((D,), jnp.float32))
    totals, key_blocks = lax.scan(accumulate, initial, (jnp.arange(block_count, dtype=jnp.int32), token_blocks, grad_blocks))
    weight_grad, gain_grad = totals
    return (key_blocks.reshape(TOKENS, KV), weight_grad, gain_grad)
```

```python
import math

import jax
import jax.numpy as jnp
from jax import lax
from jax.sharding import PartitionSpec as P

KH = 4
HD = 128
KV = 512
SEQ = 4096

rope_base = 500000.0
norm_eps = 1e-05


def rope_tables(first_row, row_count, head_size):
    position = ((first_row + jnp.arange(row_count, dtype=jnp.int32)) % SEQ).astype(jnp.float32)
    halves = jnp.arange(head_size // 2, dtype=jnp.float32)
    frequency = rope_base ** (-2.0 * halves / head_size)
    angle = position[:, None] * frequency[None, :]
    return (jnp.cos(angle), jnp.sin(angle))


def rotate(values, cosine, sine_table):
    rows = values.shape[0]
    heads = values.reshape(rows, KH, HD)
    front_half = heads[:, :, : HD // 2]
    back_half = heads[:, :, HD // 2 :]
    cosine = cosine[:, None, :]
    sine_table = sine_table[:, None, :]
    joined = jnp.concatenate(
        [
            front_half * cosine - back_half * sine_table,
            back_half * cosine + front_half * sine_table,
        ],
        axis=2,
    )
    return joined.reshape(rows, KV)


def local(tokens, norm_gain, key_weight, key_grad):
    row_count = tokens.shape[0]
    narrow_size = lax.axis_size("narrow")
    wide_size = lax.axis_size("wide")
    first_row = (lax.axis_index("wide") * narrow_size + lax.axis_index("narrow")) * row_count
    grad_scale = 1.0 / math.sqrt(row_count * narrow_size * wide_size)
    gain_col = norm_gain.astype(jnp.float32)[:, None]
    gained = (gain_col * key_weight.astype(jnp.float32)).astype(jnp.bfloat16)
    gained_wide = lax.all_gather(gained, "narrow", axis=0, tiled=True)
    widened = tokens.astype(jnp.float32)
    inv_rms = lax.rsqrt(jnp.mean(widened * widened, axis=1, keepdims=True) + norm_eps)
    cosine, sine_table = rope_tables(first_row, row_count, HD)
    pre_grad = rotate(key_grad.astype(jnp.float32), cosine, -sine_table)
    scaled_grad = (pre_grad * inv_rms).astype(jnp.bfloat16)
    part = lax.dot_general(
        tokens, scaled_grad, (((0,), (0,)), ((), ())), preferred_element_type=jnp.float32
    ).astype(jnp.bfloat16)
    part = part.reshape(narrow_size, part.shape[0] // narrow_size, KV)
    recv = lax.all_to_all(part, "narrow", split_axis=0, concat_axis=0, tiled=True)
    rows = jnp.sum(recv.astype(jnp.float32), axis=0) * grad_scale
    total = lax.psum(rows, "wide")
    projected = jnp.dot(tokens, gained_wide, preferred_element_type=jnp.float32) * inv_rms
    keys = rotate(projected, cosine, sine_table).astype(jnp.bfloat16)
    weight_grad = total * gain_col
    gain_grad = jnp.sum(total * key_weight.astype(jnp.float32), axis=1)
    return (keys, weight_grad, gain_grad)


def solution(mesh):
    return jax.shard_map(
        local,
        mesh=mesh,
        in_specs=(
            P(("wide", "narrow"), None),
            P("narrow"),
            P("narrow", None),
            P(("wide", "narrow"), None),
        ),
        out_specs=(P(("wide", "narrow"), None), P("narrow", None), P("narrow")),
        check_vma=False,
    )
```

```python
import functools
import math

import jax
import jax.numpy as jnp
from jax import lax
from jax.experimental import pallas as pl
from jax.experimental.pallas import tpu as pltpu
from jax.sharding import PartitionSpec as P

KH = 4
HD = 128
KV = 512
SEQ = 4096
Y_LO = 4
ROWS = 128

rope_base = 500000.0
norm_eps = 1e-05
MESH = pl.DeviceIdType.MESH
F32 = jnp.float32
BF16 = jnp.bfloat16


def chain_lengths(size):
    return (size // 2, size - 1 - size // 2)


def kernel(
    nx, nz, scale,
    tokens_hbm, gained_ref, key_grad_ref, cos_ref, sin_ref, weight_ref, gain_ref,
    keys_ref, weight_grad_ref, gain_grad_ref,
    tok, mixed, grads, gathered, part_y, part_z, chain_y, chain_z,
    out_x, in_x, in_z, out_y, in_y, final_y, final_z,
    local_sem, own_sem, pair_send, pair_recv, cross_send, cross_recv, far_send, far_recv,
    ring_send, ring_recv, chain_send, chain_recv,
    x_send, x_recv, z_send, z_recv, y_send, y_recv, fy_send, fy_recv, fz_send, fz_recv,
):
    ny = 2 * Y_LO
    wide = lax.axis_index("wide")
    narrow = lax.axis_index("narrow")
    core = lax.rem(narrow, 2)
    px = lax.rem(narrow // 2, nx)
    y_hi = narrow // (2 * nx)
    y_lo = lax.rem(wide, Y_LO)
    pz = wide // Y_LO
    py = y_hi * Y_LO + y_lo
    ry = ROWS // Y_LO
    rz = ROWS // nz
    blocks = 2 * nx

    def device(x, y, z, c):
        return (z * Y_LO + lax.rem(y, Y_LO), ((y // Y_LO) * nx + x) * 2 + c)

    def at_x(k):
        return device(lax.rem(px + k + nx, nx), py, pz, core)

    def at_y(k):
        return device(px, lax.rem(py + k + ny, ny), pz, core)

    def at_z(k):
        return device(px, py, lax.rem(pz + k + nz, nz), core)

    sibling = device(px, py, pz, 1 - core)
    started = []

    def remote(src, dst, send_sem, recv_sem, target):
        return pltpu.make_async_remote_copy(
            src_ref=src, dst_ref=dst, send_sem=send_sem, recv_sem=recv_sem,
            device_id=target, device_id_type=MESH,
        )

    def send(src, dst, send_sem, recv_sem, target):
        copy = remote(src, dst, send_sem, recv_sem, target)
        copy.start()
        started.append(copy)
        return copy

    def slot(hi, x, c):
        return pl.ds(pl.multiple_of(((hi * nx + x) * 2 + c) * ROWS, ROWS), ROWS)

    load = pltpu.make_async_copy(tokens_hbm, tok, local_sem)
    load.start()
    own_rows = pl.ds(pl.multiple_of(core * ROWS, ROWS), ROWS)
    own_loads = []
    for j in range(blocks):
        cols = pl.ds(pl.multiple_of((2 * j + core) * ROWS, ROWS), ROWS)
        copy = pltpu.make_async_copy(tokens_hbm.at[:, cols], mixed.at[j, own_rows, :], own_sem.at[j])
        copy.start()
        own_loads.append(copy)

    barrier = pltpu.get_barrier_semaphore()
    partners = [at_x(k) for k in range(1, nx)] + [at_y(k) for k in range(1, ny)]
    partners += [at_z(k) for k in range(1, nz)] + [sibling]
    for partner in partners:
        pl.semaphore_signal(barrier, inc=1, device_id=partner, device_id_type=MESH)

    gathered[slot(y_hi, px, core), :] = gained_ref[...]
    load.wait()
    squares = jnp.zeros((ROWS, 128), F32)
    for j in range(2 * blocks):
        piece = tok[:, j * 128 : (j + 1) * 128].astype(F32)
        squares = squares + piece * piece
    mean = jnp.sum(squares, axis=1, keepdims=True) * (1.0 / tok.shape[1])
    inv_rms = lax.rsqrt(mean + norm_eps)
    cosine, sine = cos_ref[...], sin_ref[...]
    for h in range(KH):
        head = key_grad_ref[:, h * HD : (h + 1) * HD].astype(F32)
        turned = head * cosine - pltpu.roll(head, HD // 2, 1) * sine
        grads[own_rows, h * HD : (h + 1) * HD] = (turned * inv_rms).astype(BF16)

    pl.semaphore_wait(barrier, len(partners))

    pair = [send(grads.at[own_rows, :], grads.at[own_rows, :], pair_send.at[blocks], pair_recv.at[blocks], sibling)]
    for j in range(blocks):
        cols = pl.ds(pl.multiple_of((2 * j + 1 - core) * ROWS, ROWS), ROWS)
        pair.append(send(tokens_hbm.at[:, cols], mixed.at[j, own_rows, :], pair_send.at[j], pair_recv.at[j], sibling))

    far_slot = slot(1 - y_hi, px, core)
    own_slot = slot(y_hi, px, core)

    def far_copies(sign):
        return [
            remote(gained_ref, gathered.at[own_slot, :], far_send.at[i], far_recv, at_y(sign * (i + 1)))
            for i in range(Y_LO // 2)
        ]

    @pl.when(y_lo == 0)
    def _():
        for copy in far_copies(-1):
            copy.start()

    @pl.when(y_lo == Y_LO - 1)
    def _():
        for copy in far_copies(1):
            copy.start()

    long_x, short_x = chain_lengths(nx)
    ring_steps = [[long_x, short_x], [short_x, long_x]]
    highs = (y_hi, 1 - y_hi)
    ring = {}
    cross = {}

    def ring_step(stream, way, t):
        sign = 1 - 2 * way
        if t > 0:
            ring[stream, way, t - 1].wait_recv()
            share(stream, lax.rem(px - sign * t + nx, nx), (-sign * t) % nx)
        if t < ring_steps[stream][way]:
            rows = slot(highs[stream], lax.rem(px - sign * t + nx, nx), core)
            src = gained_ref if (t == 0 and stream == 0) else gathered.at[rows, :]
            index = (stream, way, t)
            ring[index] = send(src, gathered.at[rows, :], ring_send.at[index], ring_recv.at[index], at_x(sign))

    def share(stream, x, offset):
        rows = slot(highs[stream], x, core)
        src = gained_ref if (offset == 0 and stream == 0) else gathered.at[rows, :]
        cross[stream, offset] = send(
            src, gathered.at[rows, :], cross_send.at[stream, offset], cross_recv.at[stream, offset], sibling
        )

    ring_step(0, 0, 0)
    ring_step(0, 1, 0)
    share(0, px, 0)

    for copy in own_loads:
        copy.wait()
    for copy in pair:
        copy.wait_recv()

    def block_step(j, carry):
        value = lax.dot_general(
            mixed[j], grads[...], (((0,), (0,)), ((), ())), preferred_element_type=F32
        ).astype(BF16)
        hi, x = j // nx, lax.rem(j, nx)
        for s in range(2):
            for i in range(Y_LO):
                part_y[s, hi * Y_LO + i, x] = value[i * ry : (i + 1) * ry, s * 128 : (s + 1) * 128]
            for i in range(nz):
                part_z[s, i, j] = value[i * rz : (i + 1) * rz, 256 + s * 128 : 256 + (s + 1) * 128]
        return carry

    lax.fori_loop(0, blocks, block_step, 0)

    axes = ((ny, py, at_y, part_y, chain_y), (nz, pz, at_z, part_z, chain_z))
    chains = {}

    def chain_steps(size, way, s):
        return chain_lengths(size)[(way + s) % 2]

    def chain_step(axis, way, s, t):
        size, place, at, part, chain = axes[axis]
        steps = chain_steps(size, way, s)
        if t >= steps:
            return
        sign = 1 - 2 * way
        goal = lax.rem(place + sign * (steps - t) + size, size)
        if t > 0:
            chains[axis, way, s, t - 1].wait_recv()
            total = part[s, goal].astype(F32) + chain[way, s, t - 1].astype(F32)
            part[s, goal] = total.astype(BF16)
        index = (axis, way, s, t)
        chains[index] = send(
            part.at[s, goal], chain.at[way, s, t], chain_send.at[index], chain_recv.at[index], at(sign)
        )

    remote(gained_ref, gathered.at[far_slot, :], far_send.at[0], far_recv, sibling).wait_recv()
    longest = max(ny, nz) // 2
    for t in range(longest):
        for s in range(2):
            for axis in range(2):
                for way in range(2):
                    chain_step(axis, way, s, t)
        if t == 0:
            share(1, px, 0)
            ring_step(1, 0, 0)
            ring_step(1, 1, 0)
        else:
            for stream in range(2):
                for way in range(2):
                    if t <= ring_steps[stream][way]:
                        ring_step(stream, way, t)

    for axis in range(2):
        size, place, _, part, chain = axes[axis]
        for s in range(2):
            total = part[s, place].astype(F32)
            for way in range(2):
                steps = chain_steps(size, way, s)
                if steps > 0:
                    chains[axis, way, s, steps - 1].wait_recv()
                    total = total + chain[way, s, steps - 1].astype(F32)
            total = total.astype(BF16)
            if axis == 0:
                out_x[:, s, :ry, :] = total
            else:
                for hi in range(2):
                    out_x[:, s, ry + hi * rz : ry + (hi + 1) * rz, :] = total[hi * nx : (hi + 1) * nx]

    to_x = []
    for k in range(1, nx):
        goal = lax.rem(px + k, nx)
        to_x.append(send(out_x.at[goal], in_x.at[k], x_send.at[k], x_recv.at[k], at_x(k)))

    for t in range(longest, long_x + 1):
        for stream in range(2):
            for way in range(2):
                if t <= ring_steps[stream][way]:
                    ring_step(stream, way, t)

    total = out_x[px].astype(F32)
    for k in range(1, nx):
        to_x[k - 1].wait_recv()
        total = total + in_x[k].astype(F32)
    total = total.astype(BF16)
    in_z[pz] = total[:, :ry, :]
    for hi in range(2):
        out_y[hi] = total[:, ry + hi * rz : ry + (hi + 1) * rz, :]
    in_y[py] = out_y[y_hi]

    to_z = []
    for k in range(1, nz):
        to_z.append(send(in_z.at[pz], in_z.at[pz], z_send.at[k], z_recv.at[k], at_z(k)))
    to_y = []
    for k in range(1, ny):
        goal = lax.rem(py + k, ny) // Y_LO
        to_y.append(send(out_y.at[goal], in_y.at[py], y_send.at[k], y_recv.at[k], at_y(k)))

    for copy in cross.values():
        copy.wait_recv()

    def project(k, total):
        cut = pl.ds(pl.multiple_of(k * 512, 512), 512)
        return total + jnp.dot(tok[:, cut], gathered[cut, :], preferred_element_type=F32)

    projected = lax.fori_loop(0, tok.shape[1] // 512, project, jnp.zeros((ROWS, KV), F32)) * inv_rms
    for h in range(KH):
        head = projected[:, h * HD : (h + 1) * HD]
        turned = head * cosine + pltpu.roll(head, HD // 2, 1) * sine
        keys_ref[:, h * HD : (h + 1) * HD] = turned.astype(BF16)

    for copy in to_z:
        copy.wait_recv()
    total = in_z[0].astype(F32)
    for k in range(1, nz):
        total = total + in_z[k].astype(F32)
    final_y[y_lo] = total
    pieces = []
    for k in range(1, Y_LO):
        target = device(px, y_hi * Y_LO + lax.rem(y_lo + k, Y_LO), pz, core)
        pieces.append(send(final_y.at[y_lo], final_y.at[y_lo], fy_send.at[k], fy_recv.at[k], target))
    for copy in to_y:
        copy.wait_recv()
    total = in_y[0].astype(F32)
    for k in range(1, ny):
        total = total + in_y[k].astype(F32)
    final_z[pz] = total
    for k in range(1, nz):
        pieces.append(send(final_z.at[pz], final_z.at[pz], fz_send.at[k], fz_recv.at[k], at_z(k)))
    for copy in pieces:
        copy.wait_recv()

    gain = gain_ref[...]
    dots = jnp.zeros((ROWS, 128), F32)
    for half, final in enumerate((final_y, final_z)):
        for s in range(2):
            value = final[:, s].reshape(ROWS, 128) * scale
            cols = slice(half * 256 + s * 128, half * 256 + (s + 1) * 128)
            weight_grad_ref[:, cols] = value * gain
            dots = dots + value * weight_ref[:, cols].astype(F32)
    column = jnp.sum(dots, axis=1, keepdims=True)
    gain_grad_ref[...] = jnp.broadcast_to(column, (ROWS, ROWS)).T[0:1, :]

    for copy in started:
        copy.wait_send()

    @pl.when(y_lo == 0)
    def _():
        for copy in far_copies(-1):
            copy.wait_send()

    @pl.when(y_lo == Y_LO - 1)
    def _():
        for copy in far_copies(1):
            copy.wait_send()


def local(tokens, norm_gain, key_weight, key_grad):
    rows, width = tokens.shape
    narrow_size = lax.axis_size("narrow")
    wide_size = lax.axis_size("wide")
    nx = narrow_size // 4
    ny = 2 * Y_LO
    nz = wide_size // Y_LO
    ry, rz = ROWS // Y_LO, ROWS // nz
    scale = 1.0 / math.sqrt(rows * narrow_size * wide_size)
    gain = norm_gain.astype(F32)[:, None]
    gained = (gain * key_weight.astype(F32)).astype(BF16)
    first_row = (lax.axis_index("wide") * narrow_size + lax.axis_index("narrow")) * rows
    position = ((first_row + jnp.arange(rows, dtype=jnp.int32)) % SEQ).astype(F32)
    halves = (jnp.arange(HD, dtype=jnp.int32) % (HD // 2)).astype(F32)
    frequency = rope_base ** (-2.0 * halves / HD)
    angle = position[:, None] * frequency[None, :]
    cosine = jnp.cos(angle)
    sine = jnp.sin(angle) * jnp.where(jnp.arange(HD) < HD // 2, -1.0, 1.0)[None, :]

    vmem = pl.BlockSpec(memory_space=pltpu.VMEM)
    dma = pltpu.SemaphoreType.DMA
    steps_x, steps_y, steps_z = nx // 2, ny // 2, nz // 2
    keys, weight_grad, gain_grad = pl.pallas_call(
        functools.partial(kernel, nx, nz, scale),
        out_shape=(
            jax.ShapeDtypeStruct((rows, KV), BF16),
            jax.ShapeDtypeStruct((ROWS, KV), F32),
            jax.ShapeDtypeStruct((1, ROWS), F32),
        ),
        in_specs=[pl.BlockSpec(memory_space=pl.ANY)] + [vmem] * 6,
        out_specs=(vmem, vmem, vmem),
        scratch_shapes=[
            pltpu.VMEM((rows, width), BF16),
            pltpu.VMEM((2 * nx, 2 * ROWS, 128), BF16),
            pltpu.VMEM((2 * ROWS, KV), BF16),
            pltpu.VMEM((width, KV), BF16),
            pltpu.VMEM((2, ny, nx, ry, 128), BF16),
            pltpu.VMEM((2, nz, 2 * nx, rz, 128), BF16),
            pltpu.VMEM((2, 2, steps_y, nx, ry, 128), BF16),
            pltpu.VMEM((2, 2, steps_z, 2 * nx, rz, 128), BF16),
            pltpu.VMEM((nx, 2, ry + 2 * rz, 128), BF16),
            pltpu.VMEM((nx, 2, ry + 2 * rz, 128), BF16),
            pltpu.VMEM((nz, 2, ry, 128), BF16),
            pltpu.VMEM((2, 2, rz, 128), BF16),
            pltpu.VMEM((ny, 2, rz, 128), BF16),
            pltpu.VMEM((Y_LO, 2, ry, 128), F32),
            pltpu.VMEM((nz, 2, rz, 128), F32),
            dma(()),
            dma((2 * nx,)),
            dma((2 * nx + 1,)), dma((2 * nx + 1,)),
            dma((2, nx)), dma((2, nx)),
            dma((max(Y_LO // 2, 1),)), dma(()),
            dma((2, 2, steps_x)), dma((2, 2, steps_x)),
            dma((2, 2, 2, max(steps_y, steps_z))), dma((2, 2, 2, max(steps_y, steps_z))),
            dma((nx,)), dma((nx,)),
            dma((nz,)), dma((nz,)),
            dma((ny,)), dma((ny,)),
            dma((Y_LO,)), dma((Y_LO,)),
            dma((nz,)), dma((nz,)),
        ],
        compiler_params=pltpu.CompilerParams(
            collective_id=0, has_side_effects=True, vmem_limit_bytes=48 * 1024 * 1024
        ),
    )(tokens, gained, key_grad, cosine, sine, key_weight, gain)
    return (keys, weight_grad, gain_grad.reshape(ROWS))


def solution(mesh):
    return jax.shard_map(
        local,
        mesh=mesh,
        in_specs=(
            P(("wide", "narrow"), None),
            P("narrow"),
            P("narrow", None),
            P(("wide", "narrow"), None),
        ),
        out_specs=(P(("wide", "narrow"), None), P("narrow", None), P("narrow")),
        check_vma=False,
    )
```

```python
import functools
import math

import jax
import jax.numpy as jnp
from jax import lax
from jax.experimental import pallas as pl
from jax.experimental.pallas import tpu as pltpu
from jax.sharding import PartitionSpec as P

KH = 4
HD = 128
KV = 512
SEQ = 4096
Y_LO = 4
ROWS = 128
PARTS = 2
RING_PLAN = {
    "mid": ((0, 1),), "start": (), 1: ((0, 2),), 2: ((0, 3), (1, 1)), 3: ((0, 4), (1, 2)),
    "end": ((1, 3),), "near": ((1, 4),), "far": (),
}

rope_base = 500000.0
norm_eps = 1e-05
MESH = pl.DeviceIdType.MESH
F32 = jnp.float32
BF16 = jnp.bfloat16


def chain_lengths(size):
    return (size // 2, size - 1 - size // 2)


def offset_groups(size):
    far_first = sorted(range(size), key=lambda o: (-min(o, size - o), o))
    count = size // PARTS
    return [far_first[g * count : (g + 1) * count] for g in range(PARTS)]


def kernel(
    nx, nz, scale,
    tokens_hbm, weight_hbm, key_grad_hbm, cos_ref, sin_ref, gain_ref,
    keys_ref, weight_grad_ref, gain_grad_ref,
    tok, mixed, weight, key_grad, turned_weight, proj, other, grads, gathered, part_y, part_z, chain_y, chain_z,
    out_x, in_x, in_z, out_y, in_y, final_y, final_z,
    local_sem, own_sem, pair_send, pair_recv, proj_send, proj_recv, far_send, far_recv,
    ring_send, ring_recv, chain_send, chain_recv,
    x_send, x_recv, z_send, z_recv, y_send, y_recv, fy_send, fy_recv, fz_send, fz_recv,
):
    ny = 2 * Y_LO
    wide = lax.axis_index("wide")
    narrow = lax.axis_index("narrow")
    core = lax.rem(narrow, 2)
    px = lax.rem(narrow // 2, nx)
    y_hi = narrow // (2 * nx)
    y_lo = lax.rem(wide, Y_LO)
    pz = wide // Y_LO
    py = y_hi * Y_LO + y_lo
    half_cols = KV // 2
    ky = half_cols // Y_LO
    kz = half_cols // nz
    groups = offset_groups(nx)
    group = nx // PARTS
    half_rows = ROWS // 2

    def device(x, y, z, c):
        return (z * Y_LO + lax.rem(y, Y_LO), ((y // Y_LO) * nx + x) * 2 + c)

    def at_x(k):
        return device(lax.rem(px + k + nx, nx), py, pz, core)

    def at_y(k):
        return device(px, lax.rem(py + k + ny, ny), pz, core)

    def at_z(k):
        return device(px, py, lax.rem(pz + k + nz, nz), core)

    sibling = device(px, py, pz, 1 - core)
    started = []

    def remote(src, dst, send_sem, recv_sem, target):
        return pltpu.make_async_remote_copy(
            src_ref=src, dst_ref=dst, send_sem=send_sem, recv_sem=recv_sem,
            device_id=target, device_id_type=MESH,
        )

    def send(src, dst, send_sem, recv_sem, target):
        copy = remote(src, dst, send_sem, recv_sem, target)
        copy.start()
        started.append(copy)
        return copy

    def shard(stream, offset, half):
        s = next(g for g in range(PARTS) if offset in groups[g])
        start = (stream * group + groups[s].index(offset)) * ROWS + half * half_rows
        return gathered.at[s, start : start + half_rows, :]

    barrier = pltpu.get_barrier_semaphore()
    partners = [sibling] + [at_x(k) for k in (1, -1)] + [at_z(k) for k in (1, -1)]
    partners += [at_y(k * sign) for k in range(1, max(Y_LO // 2, 1) + 1) for sign in (1, -1)]
    for partner in partners:
        pl.semaphore_signal(barrier, inc=1, device_id=partner, device_id_type=MESH)

    loads = []
    for i, (src, dst) in enumerate(((tokens_hbm, tok), (key_grad_hbm, key_grad), (weight_hbm, weight))):
        copy = pltpu.make_async_copy(src, dst, local_sem.at[i])
        copy.start()
        loads.append(copy)
    own_rows = pl.ds(pl.multiple_of(core * ROWS, ROWS), ROWS)

    highs = (y_hi, 1 - y_hi)

    def block_cols(stream, offset, c):
        hi = highs[stream]
        x = lax.rem(px + offset, nx)
        return pl.ds(pl.multiple_of(((hi * nx + x) * 2 + c) * ROWS, ROWS), ROWS)

    own_loads = {}
    for s in range(PARTS):
        for stream in range(2):
            for i, offset in enumerate(groups[s]):
                b = stream * group + i
                copy = pltpu.make_async_copy(
                    tokens_hbm.at[:, block_cols(stream, offset, core)],
                    mixed.at[s, own_rows, b * 128 : (b + 1) * 128],
                    own_sem.at[s, b],
                )
                copy.start()
                own_loads[s, b] = copy

    pl.semaphore_wait(barrier, len(partners))

    pair = {}
    for s in range(PARTS):
        for stream in range(2):
            for i, offset in enumerate(groups[s]):
                b = stream * group + i
                pair[s, b] = send(
                    tokens_hbm.at[:, block_cols(stream, offset, 1 - core)],
                    mixed.at[s, own_rows, b * 128 : (b + 1) * 128],
                    pair_send.at[s, b], pair_recv.at[s, b], sibling,
                )

    loads[2].wait()
    gain_cols = jnp.broadcast_to(gain_ref[...], (ROWS, ROWS)).T
    for h in range(KH):
        part = (weight[:, h * HD : (h + 1) * HD].astype(F32) * gain_cols).astype(BF16)
        for half in range(2):
            shard(0, 0, half)[:, h * HD : (h + 1) * HD] = part[half * half_rows : (half + 1) * half_rows]

    def far_copies(sign):
        return [
            remote(
                shard(0, 0, half), shard(1, 0, half),
                far_send.at[i, half], far_recv.at[half], at_y(sign * (i + 1)),
            )
            for half in range(2)
            for i in range(Y_LO // 2)
        ]

    @pl.when(y_lo == 0)
    def _():
        for copy in far_copies(-1):
            copy.start()

    @pl.when(y_lo == Y_LO - 1)
    def _():
        for copy in far_copies(1):
            copy.start()

    long_x, short_x = chain_lengths(nx)
    ring_steps = [[long_x, short_x], [short_x, long_x]]
    ring = {}

    def ring_step(stream, way, t, half):
        steps = ring_steps[stream][way]
        if t > steps or steps == 0:
            return
        sign = 1 - 2 * way
        if t > 0:
            ring[stream, way, t - 1, half].wait_recv()
        if t < steps:
            index = (stream, way, t, half)
            ring[index] = send(
                shard(stream, (-sign * t) % nx, half), shard(stream, (-sign * (t + 1)) % nx, half),
                ring_send.at[index], ring_recv.at[index], at_x(sign),
            )

    def ring_round(stream, t):
        for half in range(2):
            for way in range(2):
                ring_step(stream, way, t, half)

    visited = set()

    def ring_point(name):
        for item in RING_PLAN[name]:
            if item not in visited:
                ring_round(*item)
                visited.add(item)

    def ring_far_start():
        for half in range(2):
            remote(
                shard(0, 0, half), shard(1, 0, half), far_send.at[0, 0], far_recv.at[half], sibling
            ).wait_recv()
            for way in range(2):
                ring_step(1, way, 0, half)

    ring_round(0, 0)

    cosine, sine = cos_ref[...], sin_ref[...]
    loads[0].wait()
    squares = jnp.zeros((ROWS, 128), F32)
    for j in range(4 * nx):
        piece = tok[:, j * 128 : (j + 1) * 128].astype(F32)
        squares = squares + piece * piece
    mean = jnp.sum(squares, axis=1, keepdims=True) * (1.0 / tok.shape[1])
    inv_rms = lax.rsqrt(mean + norm_eps)
    loads[1].wait()
    for h in range(KH):
        part = key_grad[:, h * HD : (h + 1) * HD].astype(F32)
        turned = (part * cosine - pltpu.roll(part, HD // 2, 1) * sine) * inv_rms
        grads[core, h * HD : (h + 1) * HD, :] = turned.T.astype(BF16)
    pair["grads"] = send(grads.at[core], grads.at[core], pair_send.at[PARTS, 0], pair_recv.at[PARTS, 0], sibling)

    axes = ((ny, py, at_y, part_y, chain_y), (nz, pz, at_z, part_z, chain_z))
    chains = {}

    def chain_steps(size, way, s):
        return chain_lengths(size)[(way + s) % 2]

    def chain_step(axis, way, s, t):
        size, place, at, part, chain = axes[axis]
        steps = chain_steps(size, way, s)
        if t >= steps:
            return
        sign = 1 - 2 * way
        goal = lax.rem(place + sign * (steps - t) + size, size)
        if t > 0:
            chains[axis, way, s, t - 1].wait_recv()
            part[s, goal] = part[s, goal] + chain[way, s, t - 1]
        index = (axis, way, s, t)
        chains[index] = send(
            part.at[s, goal], chain.at[way, s, t], chain_send.at[index], chain_recv.at[index], at(sign)
        )

    def chain_round(s, t):
        for axis in range(2):
            for way in range(2):
                chain_step(axis, way, s, t)

    pair["grads"].wait_recv()
    both = jnp.concatenate([grads[0], grads[1]], axis=1)
    for s in range(PARTS):
        for b in range(2 * group):
            own_loads[s, b].wait()
            pair[s, b].wait_recv()
        for p in range(group):
            value = jnp.dot(both, mixed[s, :, p * 256 : (p + 1) * 256], preferred_element_type=F32).astype(BF16)
            for side in range(2):
                b = 2 * p + side
                stream, i = divmod(b, group)
                block = value[:, side * 128 : (side + 1) * 128]
                for k in range(Y_LO):
                    part_y[s, highs[stream] * Y_LO + k, i] = block[k * ky : (k + 1) * ky]
                for k in range(nz):
                    part_z[s, k, b] = block[half_cols + k * kz : half_cols + (k + 1) * kz]
        chain_round(s, 0)
        if s == 0:
            ring_point("mid")
    ring_far_start()
    ring_point("start")

    to_x = {}

    def chain_end(s):
        for axis in range(2):
            size, place, _, part, chain = axes[axis]
            total = part[s, place].astype(F32)
            for way in range(2):
                steps = chain_steps(size, way, s)
                if steps > 0:
                    chains[axis, way, s, steps - 1].wait_recv()
                    total = total + chain[way, s, steps - 1].astype(F32)
            total = total.astype(BF16)
            for i, offset in enumerate(groups[s]):
                if axis == 0:
                    out_x[offset, :ky, :] = total[i]
                else:
                    for hi in range(2):
                        out_x[offset, ky + hi * kz : ky + (hi + 1) * kz, :] = total[hi * group + i]
        for offset in groups[s]:
            if offset:
                to_x[offset] = send(
                    out_x.at[offset], in_x.at[offset], x_send.at[offset], x_recv.at[offset], at_x(offset)
                )

    longest = max(ny, nz) // 2
    for t in range(1, longest):
        for s in range(PARTS):
            chain_round(s, t)
        ring_point(t)
    for t in range(1, nx):
        if (0, t) not in visited:
            ring_round(0, t)
            visited.add((0, t))
    for s in range(PARTS):
        chain_end(s)
    ring_point("end")

    def project(s):
        value = jnp.dot(mixed[s], gathered[s], preferred_element_type=F32).reshape(2, ROWS, KV)
        if s == PARTS - 1:
            proj[...] = value
        else:
            proj[...] += value

    for s in range(PARTS - 1, 0, -1):
        project(s)
    ring_point("near")

    total = out_x[0].astype(F32)
    for k in range(1, nx):
        to_x[k].wait_recv()
        total = total + in_x[k].astype(F32)
    total = total.astype(BF16)
    in_z[pz] = total[:ky]
    for hi in range(2):
        out_y[hi] = total[ky + hi * kz : ky + (hi + 1) * kz]
    in_y[py] = out_y[0]

    to_z = []
    for k in range(1, nz):
        to_z.append(send(in_z.at[pz], in_z.at[pz], z_send.at[k], z_recv.at[k], at_z(k)))
    to_y = []
    for k in range(1, ny):
        goal = lax.rem(lax.rem(py + k, ny) // Y_LO + y_hi, 2)
        to_y.append(send(out_y.at[goal], in_y.at[py], y_send.at[k], y_recv.at[k], at_y(k)))

    ring_point("far")
    for stream in range(2):
        for t in range(1, nx):
            if (stream, t) not in visited:
                ring_round(stream, t)
    project(0)
    halves = send(proj.at[1 - core], other, proj_send, proj_recv, sibling)
    for h in range(KH):
        turned_weight[h * HD : (h + 1) * HD, :] = weight[:, h * HD : (h + 1) * HD].astype(F32).T

    for copy in to_z:
        copy.wait_recv()
    total = in_z[0].astype(F32)
    for k in range(1, nz):
        total = total + in_z[k].astype(F32)
    final_y[y_lo] = total.astype(BF16)
    pieces = []
    for k in range(1, Y_LO):
        target = device(px, y_hi * Y_LO + lax.rem(y_lo + k, Y_LO), pz, core)
        pieces.append(send(final_y.at[y_lo], final_y.at[y_lo], fy_send.at[k], fy_recv.at[k], target))
    for copy in to_y:
        copy.wait_recv()
    total = in_y[0].astype(F32)
    for k in range(1, ny):
        total = total + in_y[k].astype(F32)
    final_z[pz] = total.astype(BF16)
    for k in range(1, nz):
        pieces.append(send(final_z.at[pz], final_z.at[pz], fz_send.at[k], fz_recv.at[k], at_z(k)))

    halves.wait_recv()
    for h in range(KH):
        cols = slice(h * HD, (h + 1) * HD)
        part = (proj[core, :, cols] + other[:, cols]) * inv_rms
        turned = part * cosine + pltpu.roll(part, HD // 2, 1) * sine
        keys_ref[:, cols] = turned.astype(BF16)

    for copy in pieces:
        copy.wait_recv()

    gain = gain_ref[...]
    dots = jnp.zeros((ROWS, 128), F32)
    for h in range(KH):
        if h < 2:
            value = final_y[h * Y_LO // 2 : (h + 1) * Y_LO // 2].reshape(HD, 128).astype(F32) * scale
        else:
            value = final_z[(h - 2) * nz // 2 : (h - 1) * nz // 2].reshape(HD, 128).astype(F32) * scale
        dots = dots + value * turned_weight[h * HD : (h + 1) * HD, :]
        weight_grad_ref[:, h * HD : (h + 1) * HD] = (value * gain).T
    gain_grad_ref[...] = jnp.sum(dots, axis=0, keepdims=True)

    for copy in started:
        copy.wait_send()

    @pl.when(y_lo == 0)
    def _():
        for copy in far_copies(-1):
            copy.wait_send()

    @pl.when(y_lo == Y_LO - 1)
    def _():
        for copy in far_copies(1):
            copy.wait_send()


def local(tokens, norm_gain, key_weight, key_grad):
    rows, width = tokens.shape
    narrow_size = lax.axis_size("narrow")
    wide_size = lax.axis_size("wide")
    nx = narrow_size // 4
    ny = 2 * Y_LO
    nz = wide_size // Y_LO
    ky, kz = KV // 2 // Y_LO, KV // 2 // nz
    group = nx // PARTS
    scale = 1.0 / math.sqrt(rows * narrow_size * wide_size)
    gain = norm_gain.astype(F32).reshape(1, ROWS)
    first_row = (lax.axis_index("wide") * narrow_size + lax.axis_index("narrow")) * rows
    position = ((first_row + jnp.arange(rows, dtype=jnp.int32)) % SEQ).astype(F32)
    halves = (jnp.arange(HD, dtype=jnp.int32) % (HD // 2)).astype(F32)
    frequency = rope_base ** (-2.0 * halves / HD)
    angle = position[:, None] * frequency[None, :]
    cosine = jnp.cos(angle)
    sine = jnp.sin(angle) * jnp.where(jnp.arange(HD) < HD // 2, -1.0, 1.0)[None, :]

    vmem = pl.BlockSpec(memory_space=pltpu.VMEM)
    hbm = pl.BlockSpec(memory_space=pltpu.HBM)
    dma = pltpu.SemaphoreType.DMA
    steps_x, steps_y, steps_z = nx // 2, ny // 2, nz // 2
    keys, weight_grad, gain_grad = pl.pallas_call(
        functools.partial(kernel, nx, nz, scale),
        out_shape=(
            jax.ShapeDtypeStruct((rows, KV), BF16),
            jax.ShapeDtypeStruct((ROWS, KV), F32),
            jax.ShapeDtypeStruct((1, ROWS), F32),
        ),
        in_specs=[hbm] * 3 + [vmem] * 3,
        out_specs=(vmem, vmem, vmem),
        scratch_shapes=[
            pltpu.VMEM((rows, width), BF16),
            pltpu.VMEM((PARTS, 2 * ROWS, 2 * group * 128), BF16),
            pltpu.VMEM((ROWS, KV), BF16),
            pltpu.VMEM((rows, KV), BF16),
            pltpu.VMEM((KV, ROWS), F32),
            pltpu.VMEM((2, ROWS, KV), F32),
            pltpu.VMEM((ROWS, KV), F32),
            pltpu.VMEM((2, KV, ROWS), BF16),
            pltpu.VMEM((PARTS, 2 * group * ROWS, KV), BF16),
            pltpu.VMEM((PARTS, ny, group, ky, 128), BF16),
            pltpu.VMEM((PARTS, nz, 2 * group, kz, 128), BF16),
            pltpu.VMEM((2, PARTS, steps_y, group, ky, 128), BF16),
            pltpu.VMEM((2, PARTS, steps_z, 2 * group, kz, 128), BF16),
            pltpu.VMEM((nx, ky + 2 * kz, 128), BF16),
            pltpu.VMEM((nx, ky + 2 * kz, 128), BF16),
            pltpu.VMEM((nz, ky, 128), BF16),
            pltpu.VMEM((2, kz, 128), BF16),
            pltpu.VMEM((ny, kz, 128), BF16),
            pltpu.VMEM((Y_LO, ky, 128), BF16),
            pltpu.VMEM((nz, kz, 128), BF16),
            dma((3,)),
            dma((PARTS, 2 * group)),
            dma((PARTS + 1, 2 * group)), dma((PARTS + 1, 2 * group)),
            dma(()), dma(()),
            dma((max(Y_LO // 2, 1), 2)), dma((2,)),
            dma((2, 2, steps_x, 2)), dma((2, 2, steps_x, 2)),
            dma((2, 2, PARTS, max(steps_y, steps_z))), dma((2, 2, PARTS, max(steps_y, steps_z))),
            dma((nx,)), dma((nx,)),
            dma((nz,)), dma((nz,)),
            dma((ny,)), dma((ny,)),
            dma((Y_LO,)), dma((Y_LO,)),
            dma((nz,)), dma((nz,)),
        ],
        compiler_params=pltpu.CompilerParams(
            collective_id=0, has_side_effects=True, vmem_limit_bytes=55_300_000
        ),
    )(tokens, key_weight, key_grad, cosine, sine, gain)
    return (keys, weight_grad, gain_grad.reshape(ROWS))


def solution(mesh):
    return jax.shard_map(
        local,
        mesh=mesh,
        in_specs=(
            P(("wide", "narrow"), None),
            P("narrow"),
            P("narrow", None),
            P(("wide", "narrow"), None),
        ),
        out_specs=(P(("wide", "narrow"), None), P("narrow", None), P("narrow")),
        check_vma=False,
    )
```

```python
import functools
import math

import jax
import jax.numpy as jnp
from jax import lax
from jax.experimental import pallas as pl
from jax.experimental.pallas import tpu as pltpu
from jax.sharding import PartitionSpec as P

KH = 4
HD = 128
KV = 512
SEQ = 4096
Y_LO = 4
ROWS = 128
PARTS = 2
PROJECT_AT = ("summed_x", "summed_x")
RING_PLAN = {
    "mid": (), "start": ((0, 1),), 1: ((0, 2),), 2: ((1, 1),), 3: ((0, 3), (1, 2)),
    "end": ((0, 4), (1, 3)), "near": (), "far": ((1, 4),),
}
LIFT_AT = (3, "end", "near", "far")

rope_base = 500000.0
norm_eps = 1e-05
MESH = pl.DeviceIdType.MESH
F32 = jnp.float32
BF16 = jnp.bfloat16


def chain_lengths(size):
    return (size // 2, size - 1 - size // 2)


def offset_groups(size):
    far_first = sorted(range(size), key=lambda o: (-min(o, size - o), o))
    count = size // PARTS
    return [far_first[g * count : (g + 1) * count] for g in range(PARTS)]


def kernel(
    nx, nz, scale,
    tokens_hbm, weight_hbm, key_grad_hbm, cos_ref, sin_ref, gain_ref,
    keys_ref, weight_grad_ref, gain_grad_ref,
    tok, mixed, weight, key_grad, turned_weight, proj, other, grads, gathered, part_y, part_z, chain_y, chain_z,
    out_x, in_x, in_z, out_y, in_y, final_y, final_z,
    local_sem, own_sem, pair_send, pair_recv, proj_send, proj_recv, far_send, far_recv,
    ring_send, ring_recv, lift_send, lift_recv, hop_sem, chain_send, chain_recv,
    x_send, x_recv, z_send, z_recv, y_send, y_recv, fy_send, fy_recv, fz_send, fz_recv,
):
    ny = 2 * Y_LO
    wide = lax.axis_index("wide")
    narrow = lax.axis_index("narrow")
    core = lax.rem(narrow, 2)
    px = lax.rem(narrow // 2, nx)
    y_hi = narrow // (2 * nx)
    y_lo = lax.rem(wide, Y_LO)
    pz = wide // Y_LO
    py = y_hi * Y_LO + y_lo
    half_cols = KV // 2
    ky = half_cols // Y_LO
    kz = half_cols // nz
    groups = offset_groups(nx)
    group = nx // PARTS
    half_rows = ROWS // 2

    def device(x, y, z, c):
        return (z * Y_LO + lax.rem(y, Y_LO), ((y // Y_LO) * nx + x) * 2 + c)

    def at_x(k):
        return device(lax.rem(px + k + nx, nx), py, pz, core)

    def at_y(k):
        return device(px, lax.rem(py + k + ny, ny), pz, core)

    def at_z(k):
        return device(px, py, lax.rem(pz + k + nz, nz), core)

    sibling = device(px, py, pz, 1 - core)
    started = []

    def remote(src, dst, send_sem, recv_sem, target):
        return pltpu.make_async_remote_copy(
            src_ref=src, dst_ref=dst, send_sem=send_sem, recv_sem=recv_sem,
            device_id=target, device_id_type=MESH,
        )

    def send(src, dst, send_sem, recv_sem, target):
        copy = remote(src, dst, send_sem, recv_sem, target)
        copy.start()
        started.append(copy)
        return copy

    parity = lax.rem(pz, 2)
    pieces_of = (2, 1)

    def shard(stream, offset, half):
        s = next(g for g in range(PARTS) if offset in groups[g])
        start = (stream * group + groups[s].index(offset)) * ROWS
        if stream == 1:
            rows = pl.ds(pl.multiple_of(start + parity * half_rows, half_rows), half_rows)
        else:
            rows = slice(start + half * half_rows, start + (half + 1) * half_rows)
        return gathered.at[s, rows, :]

    barrier = pltpu.get_barrier_semaphore()
    partners = [sibling] + [at_x(k) for k in (1, -1)] + [at_z(k) for k in (1, -1)]
    partners += [at_y(k * sign) for k in range(1, max(Y_LO // 2, 1) + 1) for sign in (1, -1)]
    for partner in partners:
        pl.semaphore_signal(barrier, inc=1, device_id=partner, device_id_type=MESH)

    loads = []
    for i, (src, dst) in enumerate(((tokens_hbm, tok), (key_grad_hbm, key_grad), (weight_hbm, weight))):
        copy = pltpu.make_async_copy(src, dst, local_sem.at[i])
        copy.start()
        loads.append(copy)
    own_rows = pl.ds(pl.multiple_of(core * ROWS, ROWS), ROWS)

    highs = (y_hi, 1 - y_hi)

    def block_cols(stream, offset, c):
        hi = highs[stream]
        x = lax.rem(px + offset, nx)
        return pl.ds(pl.multiple_of(((hi * nx + x) * 2 + c) * ROWS, ROWS), ROWS)

    own_loads = {}
    for s in range(PARTS):
        for stream in range(2):
            for i, offset in enumerate(groups[s]):
                b = stream * group + i
                copy = pltpu.make_async_copy(
                    tokens_hbm.at[:, block_cols(stream, offset, core)],
                    mixed.at[s, own_rows, b * 128 : (b + 1) * 128],
                    own_sem.at[s, b],
                )
                copy.start()
                own_loads[s, b] = copy

    pl.semaphore_wait(barrier, len(partners))

    rounds = nx // 2 - 1
    passed = [0]

    def pass_on(upto):
        while passed[0] < upto:
            r = passed[0]
            pl.semaphore_wait(hop_sem.at[r], 2)
            passed[0] = r + 1
            if r + 1 < rounds:
                greet(r + 1)

    def greet(r):
        for k in (1, -1):
            pl.semaphore_signal(hop_sem.at[r], inc=1, device_id=at_x(k), device_id_type=MESH)

    if rounds > 0:
        greet(0)

    pair = {}
    for s in range(PARTS):
        for stream in range(2):
            for i, offset in enumerate(groups[s]):
                b = stream * group + i
                pair[s, b] = send(
                    tokens_hbm.at[:, block_cols(stream, offset, 1 - core)],
                    mixed.at[s, own_rows, b * 128 : (b + 1) * 128],
                    pair_send.at[s, b], pair_recv.at[s, b], sibling,
                )

    cosine, sine = cos_ref[...], sin_ref[...]
    loads[0].wait()
    squares = jnp.zeros((ROWS, 128), F32)
    for j in range(4 * nx):
        piece = tok[:, j * 128 : (j + 1) * 128].astype(F32)
        squares = squares + piece * piece
    mean = jnp.sum(squares, axis=1, keepdims=True) * (1.0 / tok.shape[1])
    inv_rms = lax.rsqrt(mean + norm_eps)
    loads[1].wait()
    for h in range(KH):
        part = key_grad[:, h * HD : (h + 1) * HD].astype(F32)
        turned = (part * cosine - pltpu.roll(part, HD // 2, 1) * sine) * inv_rms
        grads[core, h * HD : (h + 1) * HD, :] = turned.T.astype(BF16)
    pair["grads"] = send(grads.at[core], grads.at[core], pair_send.at[PARTS, 0], pair_recv.at[PARTS, 0], sibling)

    loads[2].wait()
    gain_cols = jnp.broadcast_to(gain_ref[...], (ROWS, ROWS)).T
    for h in range(KH):
        part = (weight[:, h * HD : (h + 1) * HD].astype(F32) * gain_cols).astype(BF16)
        for half in range(2):
            shard(0, 0, half)[:, h * HD : (h + 1) * HD] = part[half * half_rows : (half + 1) * half_rows]

    own_half = gathered.at[
        PARTS - 1,
        pl.ds(pl.multiple_of(groups[PARTS - 1].index(0) * ROWS + parity * half_rows, half_rows), half_rows),
        :,
    ]

    def far_copies(sign):
        return [
            remote(own_half, shard(1, 0, 0), far_send.at[i], far_recv, at_y(sign * (i + 1)))
            for i in range(Y_LO // 2)
        ]

    @pl.when(y_lo == 0)
    def _():
        for copy in far_copies(-1):
            copy.start()

    @pl.when(y_lo == Y_LO - 1)
    def _():
        for copy in far_copies(1):
            copy.start()

    long_x, short_x = chain_lengths(nx)
    ring_steps = [[long_x, short_x], [short_x, long_x]]
    ring = {}

    def ring_step(stream, way, t, half):
        steps = ring_steps[stream][way]
        if t > steps or steps == 0:
            return
        sign = 1 - 2 * way
        if t > 0:
            ring[stream, way, t - 1, half].wait_recv()
        if t < steps:
            index = (stream, way, t, half)
            ring[index] = send(
                shard(stream, (-sign * t) % nx, half), shard(stream, (-sign * (t + 1)) % nx, half),
                ring_send.at[index], ring_recv.at[index], at_x(sign),
            )

    lifts = {}
    waiting = []

    def lift(offset):
        rows = shard(1, offset, 0)
        toward = 1 - 2 * (next(g.index(offset) for g in groups if offset in g) % 2)
        lifts[offset] = send(rows, rows, lift_send.at[offset], lift_recv.at[offset], at_z(toward))

    def ring_round(stream, t):
        for half in range(pieces_of[stream]):
            for way in range(2):
                ring_step(stream, way, t, half)
                if stream == 1 and 0 < t <= ring_steps[1][way]:
                    waiting.append((-(1 - 2 * way) * t) % nx)

    visited = set()

    def ring_point(name):
        for item in RING_PLAN[name]:
            if item not in visited:
                ring_round(*item)
                visited.add(item)
        while waiting and name in LIFT_AT:
            lift(waiting.pop(0))

    def ring_far_start():
        remote(own_half, shard(1, 0, 0), far_send.at[0], far_recv, sibling).wait_recv()
        for way in range(2):
            ring_step(1, way, 0, 0)
        waiting.append(0)

    ring_round(0, 0)

    axes = ((ny, py, at_y, part_y, chain_y), (nz, pz, at_z, part_z, chain_z))
    chains = {}

    def chain_steps(size, way, s):
        return chain_lengths(size)[(way + s) % 2]

    def chain_step(axis, way, s, t):
        size, place, at, part, chain = axes[axis]
        steps = chain_steps(size, way, s)
        if t >= steps:
            return
        sign = 1 - 2 * way
        goal = lax.rem(place + sign * (steps - t) + size, size)
        if t > 0:
            chains[axis, way, s, t - 1].wait_recv()
            part[s, goal] = part[s, goal] + chain[way, s, t - 1]
        index = (axis, way, s, t)
        chains[index] = send(
            part.at[s, goal], chain.at[way, s, t], chain_send.at[index], chain_recv.at[index], at(sign)
        )

    def chain_round(s, t):
        for axis in range(2):
            for way in range(2):
                chain_step(axis, way, s, t)

    pair["grads"].wait_recv()
    both = jnp.concatenate([grads[0], grads[1]], axis=1)
    for s in range(PARTS):
        for b in range(2 * group):
            own_loads[s, b].wait()
            pair[s, b].wait_recv()
        for p in range(group):
            value = jnp.dot(both, mixed[s, :, p * 256 : (p + 1) * 256], preferred_element_type=F32).astype(BF16)
            for side in range(2):
                b = 2 * p + side
                stream, i = divmod(b, group)
                block = value[:, side * 128 : (side + 1) * 128]
                for k in range(Y_LO):
                    part_y[s, highs[stream] * Y_LO + k, i] = block[k * ky : (k + 1) * ky]
                for k in range(nz):
                    part_z[s, k, b] = block[half_cols + k * kz : half_cols + (k + 1) * kz]
        chain_round(s, 0)
        pass_on(min(s + 1, rounds))
        if s == 0:
            ring_point("mid")
    ring_far_start()
    ring_point("start")

    to_x = {}

    def chain_end(s):
        for axis in range(2):
            size, place, _, part, chain = axes[axis]
            total = part[s, place].astype(F32)
            for way in range(2):
                steps = chain_steps(size, way, s)
                if steps > 0:
                    chains[axis, way, s, steps - 1].wait_recv()
                    total = total + chain[way, s, steps - 1].astype(F32)
            total = total.astype(BF16)
            for i, offset in enumerate(groups[s]):
                if axis == 0:
                    out_x[offset, :ky, :] = total[i]
                else:
                    for hi in range(2):
                        out_x[offset, ky + hi * kz : ky + (hi + 1) * kz, :] = total[hi * group + i]
        for offset in groups[s]:
            if offset:
                to_x[offset] = send(
                    out_x.at[offset], in_x.at[offset], x_send.at[offset], x_recv.at[offset], at_x(offset)
                )

    longest = max(ny, nz) // 2
    for t in range(1, longest):
        for s in range(PARTS):
            chain_round(s, t)
        ring_point(t)
    pass_on(rounds)
    for s in range(PARTS):
        chain_end(s)
    ring_point("end")

    def project(s):
        for offset in groups[s]:
            lifts[offset].wait_recv()
        value = jnp.dot(mixed[s], gathered[s], preferred_element_type=F32).reshape(2, ROWS, KV)
        if s == PARTS - 1:
            proj[...] = value
        else:
            proj[...] += value

    ring_point("near")

    def ring_rest():
        for stream in range(2):
            for t in range(1, nx):
                if (stream, t) not in visited:
                    visited.add((stream, t))
                    ring_round(stream, t)
        while waiting:
            lift(waiting.pop(0))

    def project_at(point):
        for s in range(PARTS - 1, -1, -1):
            if PROJECT_AT[s] == point:
                if s == 0 or point == "summed_all":
                    ring_point("far")
                    ring_rest()
                project(s)
                if s == 0:
                    proj_copy.append(
                        send(proj.at[1 - core], other, proj_send, proj_recv, sibling)
                    )

    proj_copy = []
    project_at("chained")

    total = out_x[0].astype(F32)
    for k in range(1, nx):
        to_x[k].wait_recv()
        total = total + in_x[k].astype(F32)
    total = total.astype(BF16)
    in_z[pz] = total[:ky]
    for hi in range(2):
        out_y[hi] = total[ky + hi * kz : ky + (hi + 1) * kz]
    in_y[py] = out_y[0]

    to_z = []
    for k in range(1, nz):
        to_z.append(send(in_z.at[pz], in_z.at[pz], z_send.at[k], z_recv.at[k], at_z(k)))
    to_y = []
    for k in range(1, ny):
        goal = lax.rem(lax.rem(py + k, ny) // Y_LO + y_hi, 2)
        to_y.append(send(out_y.at[goal], in_y.at[py], y_send.at[k], y_recv.at[k], at_y(k)))

    project_at("summed_x")
    for h in range(KH):
        turned_weight[h * HD : (h + 1) * HD, :] = weight[:, h * HD : (h + 1) * HD].astype(F32).T

    for copy in to_z:
        copy.wait_recv()
    total = in_z[0].astype(F32)
    for k in range(1, nz):
        total = total + in_z[k].astype(F32)
    final_y[y_lo] = total.astype(BF16)
    pieces = []
    for k in range(1, Y_LO):
        target = device(px, y_hi * Y_LO + lax.rem(y_lo + k, Y_LO), pz, core)
        pieces.append(send(final_y.at[y_lo], final_y.at[y_lo], fy_send.at[k], fy_recv.at[k], target))
    for copy in to_y:
        copy.wait_recv()
    total = in_y[0].astype(F32)
    for k in range(1, ny):
        total = total + in_y[k].astype(F32)
    final_z[pz] = total.astype(BF16)
    for k in range(1, nz):
        pieces.append(send(final_z.at[pz], final_z.at[pz], fz_send.at[k], fz_recv.at[k], at_z(k)))

    project_at("summed_all")
    proj_copy[0].wait_recv()
    for h in range(KH):
        cols = slice(h * HD, (h + 1) * HD)
        part = (proj[core, :, cols] + other[:, cols]) * inv_rms
        turned = part * cosine + pltpu.roll(part, HD // 2, 1) * sine
        keys_ref[:, cols] = turned.astype(BF16)

    for copy in pieces:
        copy.wait_recv()

    gain = gain_ref[...]
    dots = jnp.zeros((ROWS, 128), F32)
    for h in range(KH):
        if h < 2:
            value = final_y[h * Y_LO // 2 : (h + 1) * Y_LO // 2].reshape(HD, 128).astype(F32) * scale
        else:
            value = final_z[(h - 2) * nz // 2 : (h - 1) * nz // 2].reshape(HD, 128).astype(F32) * scale
        dots = dots + value * turned_weight[h * HD : (h + 1) * HD, :]
        weight_grad_ref[:, h * HD : (h + 1) * HD] = (value * gain).T
    gain_grad_ref[...] = jnp.sum(dots, axis=0, keepdims=True)

    for copy in started:
        copy.wait_send()

    @pl.when(y_lo == 0)
    def _():
        for copy in far_copies(-1):
            copy.wait_send()

    @pl.when(y_lo == Y_LO - 1)
    def _():
        for copy in far_copies(1):
            copy.wait_send()


def local(tokens, norm_gain, key_weight, key_grad):
    rows, width = tokens.shape
    narrow_size = lax.axis_size("narrow")
    wide_size = lax.axis_size("wide")
    nx = narrow_size // 4
    ny = 2 * Y_LO
    nz = wide_size // Y_LO
    ky, kz = KV // 2 // Y_LO, KV // 2 // nz
    group = nx // PARTS
    scale = 1.0 / math.sqrt(rows * narrow_size * wide_size)
    gain = norm_gain.astype(F32).reshape(1, ROWS)
    first_row = (lax.axis_index("wide") * narrow_size + lax.axis_index("narrow")) * rows
    position = ((first_row + jnp.arange(rows, dtype=jnp.int32)) % SEQ).astype(F32)
    halves = (jnp.arange(HD, dtype=jnp.int32) % (HD // 2)).astype(F32)
    frequency = rope_base ** (-2.0 * halves / HD)
    angle = position[:, None] * frequency[None, :]
    cosine = jnp.cos(angle)
    sine = jnp.sin(angle) * jnp.where(jnp.arange(HD) < HD // 2, -1.0, 1.0)[None, :]

    vmem = pl.BlockSpec(memory_space=pltpu.VMEM)
    hbm = pl.BlockSpec(memory_space=pltpu.HBM)
    dma = pltpu.SemaphoreType.DMA
    steps_x, steps_y, steps_z = nx // 2, ny // 2, nz // 2
    keys, weight_grad, gain_grad = pl.pallas_call(
        functools.partial(kernel, nx, nz, scale),
        out_shape=(
            jax.ShapeDtypeStruct((rows, KV), BF16),
            jax.ShapeDtypeStruct((ROWS, KV), F32),
            jax.ShapeDtypeStruct((1, ROWS), F32),
        ),
        in_specs=[hbm] * 3 + [vmem] * 3,
        out_specs=(vmem, vmem, vmem),
        scratch_shapes=[
            pltpu.VMEM((rows, width), BF16),
            pltpu.VMEM((PARTS, 2 * ROWS, 2 * group * 128), BF16),
            pltpu.VMEM((ROWS, KV), BF16),
            pltpu.VMEM((rows, KV), BF16),
            pltpu.VMEM((KV, ROWS), F32),
            pltpu.VMEM((2, ROWS, KV), F32),
            pltpu.VMEM((ROWS, KV), F32),
            pltpu.VMEM((2, KV, ROWS), BF16),
            pltpu.VMEM((PARTS, 2 * group * ROWS, KV), BF16),
            pltpu.VMEM((PARTS, ny, group, ky, 128), BF16),
            pltpu.VMEM((PARTS, nz, 2 * group, kz, 128), BF16),
            pltpu.VMEM((2, PARTS, steps_y, group, ky, 128), BF16),
            pltpu.VMEM((2, PARTS, steps_z, 2 * group, kz, 128), BF16),
            pltpu.VMEM((nx, ky + 2 * kz, 128), BF16),
            pltpu.VMEM((nx, ky + 2 * kz, 128), BF16),
            pltpu.VMEM((nz, ky, 128), BF16),
            pltpu.VMEM((2, kz, 128), BF16),
            pltpu.VMEM((ny, kz, 128), BF16),
            pltpu.VMEM((Y_LO, ky, 128), BF16),
            pltpu.VMEM((nz, kz, 128), BF16),
            dma((3,)),
            dma((PARTS, 2 * group)),
            dma((PARTS + 1, 2 * group)), dma((PARTS + 1, 2 * group)),
            dma(()), dma(()),
            dma((max(Y_LO // 2, 1),)), dma(()),
            dma((2, 2, steps_x, 2)), dma((2, 2, steps_x, 2)),
            dma((nx,)), dma((nx,)),
            pltpu.SemaphoreType.REGULAR((max(nx // 2 - 1, 1),)),
            dma((2, 2, PARTS, max(steps_y, steps_z))), dma((2, 2, PARTS, max(steps_y, steps_z))),
            dma((nx,)), dma((nx,)),
            dma((nz,)), dma((nz,)),
            dma((ny,)), dma((ny,)),
            dma((Y_LO,)), dma((Y_LO,)),
            dma((nz,)), dma((nz,)),
        ],
        compiler_params=pltpu.CompilerParams(
            collective_id=0, has_side_effects=True, vmem_limit_bytes=55_300_000
        ),
    )(tokens, key_weight, key_grad, cosine, sine, gain)
    return (keys, weight_grad, gain_grad.reshape(ROWS))


def solution(mesh):
    return jax.shard_map(
        local,
        mesh=mesh,
        in_specs=(
            P(("wide", "narrow"), None),
            P("narrow"),
            P("narrow", None),
            P(("wide", "narrow"), None),
        ),
        out_specs=(P(("wide", "narrow"), None), P("narrow", None), P("narrow")),
        check_vma=False,
    )
```

```python
import functools
import math

import jax
import jax.numpy as jnp
from jax import lax
from jax.experimental import pallas as pl
from jax.experimental.pallas import tpu as pltpu
from jax.sharding import PartitionSpec as P

KH = 4
HD = 128
KV = 512
SEQ = 4096
Y_LO = 4
ROWS = 128
PARTS = 2
PROJECT_AT = ("summed_x", "summed_x")
RING_PLAN = {
    "mid": (), "start": ((0, 1),), 1: ((0, 2),), 2: ((1, 1), (0, 3)), 3: ((1, 2),),
    "end": ((0, 4), (1, 3)), "near": (), "far": ((1, 4),),
}
LIFT_AT = (3, "end", "near", "far")

rope_base = 500000.0
norm_eps = 1e-05
MESH = pl.DeviceIdType.MESH
F32 = jnp.float32
BF16 = jnp.bfloat16


def chain_lengths(size):
    return (size // 2, size - 1 - size // 2)


def offset_groups(size):
    far_first = sorted(range(size), key=lambda o: (-min(o, size - o), o))
    count = size // PARTS
    return [far_first[g * count : (g + 1) * count] for g in range(PARTS)]


def kernel(
    nx, nz, scale,
    tokens_hbm, weight_hbm, key_grad_hbm, cos_ref, sin_ref, gain_ref,
    keys_ref, weight_grad_ref, gain_grad_ref,
    tok, mixed, weight, key_grad, turned_weight, proj, other, grads, gathered, part_y, part_z, chain_y, chain_z,
    out_x, in_x, in_z, out_y, in_y, final_y, final_z,
    local_sem, own_sem, pair_send, pair_recv, proj_send, proj_recv, far_send, far_recv,
    ring_send, ring_recv, lift_send, lift_recv, hop_sem, chain_send, chain_recv,
    x_send, x_recv, z_send, z_recv, y_send, y_recv, fy_send, fy_recv, fz_send, fz_recv,
):
    ny = 2 * Y_LO
    wide = lax.axis_index("wide")
    narrow = lax.axis_index("narrow")
    core = lax.rem(narrow, 2)
    px = lax.rem(narrow // 2, nx)
    y_hi = narrow // (2 * nx)
    y_lo = lax.rem(wide, Y_LO)
    pz = wide // Y_LO
    py = y_hi * Y_LO + y_lo
    half_cols = KV // 2
    ky = half_cols // Y_LO
    kz = half_cols // nz
    groups = offset_groups(nx)
    group = nx // PARTS
    half_rows = ROWS // 2

    def device(x, y, z, c):
        return (z * Y_LO + lax.rem(y, Y_LO), ((y // Y_LO) * nx + x) * 2 + c)

    def at_x(k):
        return device(lax.rem(px + k + nx, nx), py, pz, core)

    def at_y(k):
        return device(px, lax.rem(py + k + ny, ny), pz, core)

    def at_z(k):
        return device(px, py, lax.rem(pz + k + nz, nz), core)

    sibling = device(px, py, pz, 1 - core)
    started = []

    def remote(src, dst, send_sem, recv_sem, target):
        return pltpu.make_async_remote_copy(
            src_ref=src, dst_ref=dst, send_sem=send_sem, recv_sem=recv_sem,
            device_id=target, device_id_type=MESH,
        )

    def send(src, dst, send_sem, recv_sem, target):
        copy = remote(src, dst, send_sem, recv_sem, target)
        copy.start()
        started.append(copy)
        return copy

    parity = lax.rem(pz, 2)
    pieces_of = (2, 1)

    def shard(stream, offset, half):
        s = next(g for g in range(PARTS) if offset in groups[g])
        start = (stream * group + groups[s].index(offset)) * ROWS
        if stream == 1:
            rows = pl.ds(pl.multiple_of(start + parity * half_rows, half_rows), half_rows)
        else:
            rows = slice(start + half * half_rows, start + (half + 1) * half_rows)
        return gathered.at[s, rows, :]

    barrier = pltpu.get_barrier_semaphore()
    partners = [sibling] + [at_x(k) for k in (1, -1)] + [at_z(k) for k in (1, -1)]
    partners += [at_y(k * sign) for k in range(1, max(Y_LO // 2, 1) + 1) for sign in (1, -1)]
    for partner in partners:
        pl.semaphore_signal(barrier, inc=1, device_id=partner, device_id_type=MESH)

    loads = []
    for i, (src, dst) in enumerate(((tokens_hbm, tok), (key_grad_hbm, key_grad), (weight_hbm, weight))):
        copy = pltpu.make_async_copy(src, dst, local_sem.at[i])
        copy.start()
        loads.append(copy)
    own_rows = pl.ds(pl.multiple_of(core * ROWS, ROWS), ROWS)

    highs = (y_hi, 1 - y_hi)

    def block_cols(stream, offset, c):
        hi = highs[stream]
        x = lax.rem(px + offset, nx)
        return pl.ds(pl.multiple_of(((hi * nx + x) * 2 + c) * ROWS, ROWS), ROWS)

    own_loads = {}
    for s in range(PARTS):
        for stream in range(2):
            for i, offset in enumerate(groups[s]):
                b = stream * group + i
                copy = pltpu.make_async_copy(
                    tokens_hbm.at[:, block_cols(stream, offset, core)],
                    mixed.at[s, own_rows, b * 128 : (b + 1) * 128],
                    own_sem.at[s, b],
                )
                copy.start()
                own_loads[s, b] = copy

    pl.semaphore_wait(barrier, len(partners))

    rounds = nx // 2 - 1
    passed = [0]

    def pass_on(upto):
        while passed[0] < upto:
            r = passed[0]
            pl.semaphore_wait(hop_sem.at[r], 2)
            passed[0] = r + 1
            if r + 1 < rounds:
                greet(r + 1)

    def greet(r):
        for k in (1, -1):
            pl.semaphore_signal(hop_sem.at[r], inc=1, device_id=at_x(k), device_id_type=MESH)

    if rounds > 0:
        greet(0)

    pair = {}
    for s in range(PARTS):
        for stream in range(2):
            for i, offset in enumerate(groups[s]):
                b = stream * group + i
                pair[s, b] = send(
                    tokens_hbm.at[:, block_cols(stream, offset, 1 - core)],
                    mixed.at[s, own_rows, b * 128 : (b + 1) * 128],
                    pair_send.at[s, b], pair_recv.at[s, b], sibling,
                )

    cosine, sine = cos_ref[...], sin_ref[...]
    loads[0].wait()
    squares = jnp.zeros((ROWS, 128), F32)
    for j in range(4 * nx):
        piece = tok[:, j * 128 : (j + 1) * 128].astype(F32)
        squares = squares + piece * piece
    mean = jnp.sum(squares, axis=1, keepdims=True) * (1.0 / tok.shape[1])
    inv_rms = lax.rsqrt(mean + norm_eps)
    loads[1].wait()
    for h in range(KH):
        part = key_grad[:, h * HD : (h + 1) * HD].astype(F32)
        turned = (part * cosine - pltpu.roll(part, HD // 2, 1) * sine) * inv_rms
        grads[core, h * HD : (h + 1) * HD, :] = turned.T.astype(BF16)
    pair["grads"] = send(grads.at[core], grads.at[core], pair_send.at[PARTS, 0], pair_recv.at[PARTS, 0], sibling)

    loads[2].wait()
    gain_cols = jnp.broadcast_to(gain_ref[...], (ROWS, ROWS)).T
    for h in range(KH):
        part = (weight[:, h * HD : (h + 1) * HD].astype(F32) * gain_cols).astype(BF16)
        for half in range(2):
            shard(0, 0, half)[:, h * HD : (h + 1) * HD] = part[half * half_rows : (half + 1) * half_rows]

    own_half = gathered.at[
        PARTS - 1,
        pl.ds(pl.multiple_of(groups[PARTS - 1].index(0) * ROWS + parity * half_rows, half_rows), half_rows),
        :,
    ]

    def far_copies(sign):
        return [
            remote(own_half, shard(1, 0, 0), far_send.at[i], far_recv, at_y(sign * (i + 1)))
            for i in range(Y_LO // 2)
        ]

    @pl.when(y_lo == 0)
    def _():
        for copy in far_copies(-1):
            copy.start()

    @pl.when(y_lo == Y_LO - 1)
    def _():
        for copy in far_copies(1):
            copy.start()

    long_x, short_x = chain_lengths(nx)
    ring_steps = [[long_x, short_x], [short_x, long_x]]
    ring = {}

    def ring_step(stream, way, t, half):
        steps = ring_steps[stream][way]
        if t > steps or steps == 0:
            return
        sign = 1 - 2 * way
        if t > 0:
            ring[stream, way, t - 1, half].wait_recv()
        if t < steps:
            index = (stream, way, t, half)
            ring[index] = send(
                shard(stream, (-sign * t) % nx, half), shard(stream, (-sign * (t + 1)) % nx, half),
                ring_send.at[index], ring_recv.at[index], at_x(sign),
            )

    lifts = {}
    waiting = []

    def lift(offset):
        rows = shard(1, offset, 0)
        toward = 1 - 2 * (next(g.index(offset) for g in groups if offset in g) % 2)
        lifts[offset] = send(rows, rows, lift_send.at[offset], lift_recv.at[offset], at_z(toward))

    def ring_round(stream, t):
        for half in range(pieces_of[stream]):
            for way in range(2):
                ring_step(stream, way, t, half)
                if stream == 1 and 0 < t <= ring_steps[1][way]:
                    waiting.append((-(1 - 2 * way) * t) % nx)

    visited = set()

    def ring_point(name):
        for item in RING_PLAN[name]:
            if item not in visited:
                ring_round(*item)
                visited.add(item)
        while waiting and name in LIFT_AT:
            lift(waiting.pop(0))

    def ring_far_start():
        remote(own_half, shard(1, 0, 0), far_send.at[0], far_recv, sibling).wait_recv()
        for way in range(2):
            ring_step(1, way, 0, 0)
        waiting.append(0)

    ring_round(0, 0)

    axes = ((ny, py, at_y, part_y, chain_y), (nz, pz, at_z, part_z, chain_z))
    chains = {}

    def chain_steps(size, way, s):
        return chain_lengths(size)[(way + s) % 2]

    def chain_step(axis, way, s, t):
        size, place, at, part, chain = axes[axis]
        steps = chain_steps(size, way, s)
        if t >= steps:
            return
        sign = 1 - 2 * way
        goal = lax.rem(place + sign * (steps - t) + size, size)
        if t > 0:
            chains[axis, way, s, t - 1].wait_recv()
            part[s, goal] = part[s, goal] + chain[way, s, t - 1]
        index = (axis, way, s, t)
        chains[index] = send(
            part.at[s, goal], chain.at[way, s, t], chain_send.at[index], chain_recv.at[index], at(sign)
        )

    def chain_round(s, t):
        for axis in range(2):
            for way in range(2):
                chain_step(axis, way, s, t)

    pair["grads"].wait_recv()
    both = jnp.concatenate([grads[0], grads[1]], axis=1)
    for s in range(PARTS):
        for b in range(2 * group):
            own_loads[s, b].wait()
            pair[s, b].wait_recv()
        for p in range(group):
            value = jnp.dot(both, mixed[s, :, p * 256 : (p + 1) * 256], preferred_element_type=F32).astype(BF16)
            for side in range(2):
                b = 2 * p + side
                stream, i = divmod(b, group)
                block = value[:, side * 128 : (side + 1) * 128]
                for k in range(Y_LO):
                    part_y[s, highs[stream] * Y_LO + k, i] = block[k * ky : (k + 1) * ky]
                for k in range(nz):
                    part_z[s, k, b] = block[half_cols + k * kz : half_cols + (k + 1) * kz]
        chain_round(s, 0)
        pass_on(min(s + 1, rounds))
        if s == 0:
            ring_point("mid")
    ring_far_start()
    ring_point("start")

    to_x = {}

    def chain_end(s):
        for axis in range(2):
            size, place, _, part, chain = axes[axis]
            total = part[s, place].astype(F32)
            for way in range(2):
                steps = chain_steps(size, way, s)
                if steps > 0:
                    chains[axis, way, s, steps - 1].wait_recv()
                    total = total + chain[way, s, steps - 1].astype(F32)
            total = total.astype(BF16)
            for i, offset in enumerate(groups[s]):
                if axis == 0:
                    out_x[offset, :ky, :] = total[i]
                else:
                    for hi in range(2):
                        out_x[offset, ky + hi * kz : ky + (hi + 1) * kz, :] = total[hi * group + i]
        for offset in groups[s]:
            if offset:
                to_x[offset] = send(
                    out_x.at[offset], in_x.at[offset], x_send.at[offset], x_recv.at[offset], at_x(offset)
                )

    longest = max(ny, nz) // 2
    for t in range(1, longest):
        for s in range(PARTS):
            chain_round(s, t)
        ring_point(t)
    pass_on(rounds)
    for s in range(PARTS):
        chain_end(s)
    ring_point("end")

    def project(s):
        for offset in groups[s]:
            lifts[offset].wait_recv()
        value = jnp.dot(mixed[s], gathered[s], preferred_element_type=F32).reshape(2, ROWS, KV)
        if s == PARTS - 1:
            proj[...] = value
        else:
            proj[...] += value

    ring_point("near")

    def ring_rest():
        for stream in range(2):
            for t in range(1, nx):
                if (stream, t) not in visited:
                    visited.add((stream, t))
                    ring_round(stream, t)
        while waiting:
            lift(waiting.pop(0))

    def project_at(point):
        for s in range(PARTS - 1, -1, -1):
            if PROJECT_AT[s] == point:
                if s == 0 or point == "summed_all":
                    ring_point("far")
                    ring_rest()
                project(s)
                if s == 0:
                    proj_copy.append(
                        send(proj.at[1 - core], other, proj_send, proj_recv, sibling)
                    )

    proj_copy = []
    project_at("chained")

    total = out_x[0].astype(F32)
    for k in range(1, nx):
        to_x[k].wait_recv()
        total = total + in_x[k].astype(F32)
    total = total.astype(BF16)
    in_z[pz] = total[:ky]
    for hi in range(2):
        out_y[hi] = total[ky + hi * kz : ky + (hi + 1) * kz]
    in_y[py] = out_y[0]

    to_z = []
    for k in range(1, nz):
        to_z.append(send(in_z.at[pz], in_z.at[pz], z_send.at[k], z_recv.at[k], at_z(k)))
    to_y = []
    for k in range(1, ny):
        goal = lax.rem(lax.rem(py + k, ny) // Y_LO + y_hi, 2)
        to_y.append(send(out_y.at[goal], in_y.at[py], y_send.at[k], y_recv.at[k], at_y(k)))

    project_at("summed_x")
    for h in range(KH):
        turned_weight[h * HD : (h + 1) * HD, :] = weight[:, h * HD : (h + 1) * HD].astype(F32).T

    for copy in to_z:
        copy.wait_recv()
    total = in_z[0].astype(F32)
    for k in range(1, nz):
        total = total + in_z[k].astype(F32)
    final_y[y_lo] = total.astype(BF16)
    pieces = []
    for k in range(1, Y_LO):
        target = device(px, y_hi * Y_LO + lax.rem(y_lo + k, Y_LO), pz, core)
        pieces.append(send(final_y.at[y_lo], final_y.at[y_lo], fy_send.at[k], fy_recv.at[k], target))
    for copy in to_y:
        copy.wait_recv()
    total = in_y[0].astype(F32)
    for k in range(1, ny):
        total = total + in_y[k].astype(F32)
    final_z[pz] = total.astype(BF16)
    for k in range(1, nz):
        pieces.append(send(final_z.at[pz], final_z.at[pz], fz_send.at[k], fz_recv.at[k], at_z(k)))

    project_at("summed_all")
    proj_copy[0].wait_recv()
    for h in range(KH):
        cols = slice(h * HD, (h + 1) * HD)
        part = (proj[core, :, cols] + other[:, cols]) * inv_rms
        turned = part * cosine + pltpu.roll(part, HD // 2, 1) * sine
        keys_ref[:, cols] = turned.astype(BF16)

    for copy in pieces:
        copy.wait_recv()

    gain = gain_ref[...]
    dots = jnp.zeros((ROWS, 128), F32)
    for h in range(KH):
        if h < 2:
            value = final_y[h * Y_LO // 2 : (h + 1) * Y_LO // 2].reshape(HD, 128).astype(F32) * scale
        else:
            value = final_z[(h - 2) * nz // 2 : (h - 1) * nz // 2].reshape(HD, 128).astype(F32) * scale
        dots = dots + value * turned_weight[h * HD : (h + 1) * HD, :]
        weight_grad_ref[:, h * HD : (h + 1) * HD] = (value * gain).T
    gain_grad_ref[...] = jnp.sum(dots, axis=0, keepdims=True)

    for copy in started:
        copy.wait_send()

    @pl.when(y_lo == 0)
    def _():
        for copy in far_copies(-1):
            copy.wait_send()

    @pl.when(y_lo == Y_LO - 1)
    def _():
        for copy in far_copies(1):
            copy.wait_send()


def local(tokens, norm_gain, key_weight, key_grad):
    rows, width = tokens.shape
    narrow_size = lax.axis_size("narrow")
    wide_size = lax.axis_size("wide")
    nx = narrow_size // 4
    ny = 2 * Y_LO
    nz = wide_size // Y_LO
    ky, kz = KV // 2 // Y_LO, KV // 2 // nz
    group = nx // PARTS
    scale = 1.0 / math.sqrt(rows * narrow_size * wide_size)
    gain = norm_gain.astype(F32).reshape(1, ROWS)
    first_row = (lax.axis_index("wide") * narrow_size + lax.axis_index("narrow")) * rows
    position = ((first_row + jnp.arange(rows, dtype=jnp.int32)) % SEQ).astype(F32)
    halves = (jnp.arange(HD, dtype=jnp.int32) % (HD // 2)).astype(F32)
    frequency = rope_base ** (-2.0 * halves / HD)
    angle = position[:, None] * frequency[None, :]
    cosine = jnp.cos(angle)
    sine = jnp.sin(angle) * jnp.where(jnp.arange(HD) < HD // 2, -1.0, 1.0)[None, :]

    vmem = pl.BlockSpec(memory_space=pltpu.VMEM)
    hbm = pl.BlockSpec(memory_space=pltpu.HBM)
    dma = pltpu.SemaphoreType.DMA
    steps_x, steps_y, steps_z = nx // 2, ny // 2, nz // 2
    keys, weight_grad, gain_grad = pl.pallas_call(
        functools.partial(kernel, nx, nz, scale),
        out_shape=(
            jax.ShapeDtypeStruct((rows, KV), BF16),
            jax.ShapeDtypeStruct((ROWS, KV), F32),
            jax.ShapeDtypeStruct((1, ROWS), F32),
        ),
        in_specs=[hbm] * 3 + [vmem] * 3,
        out_specs=(vmem, vmem, vmem),
        scratch_shapes=[
            pltpu.VMEM((rows, width), BF16),
            pltpu.VMEM((PARTS, 2 * ROWS, 2 * group * 128), BF16),
            pltpu.VMEM((ROWS, KV), BF16),
            pltpu.VMEM((rows, KV), BF16),
            pltpu.VMEM((KV, ROWS), F32),
            pltpu.VMEM((2, ROWS, KV), F32),
            pltpu.VMEM((ROWS, KV), F32),
            pltpu.VMEM((2, KV, ROWS), BF16),
            pltpu.VMEM((PARTS, 2 * group * ROWS, KV), BF16),
            pltpu.VMEM((PARTS, ny, group, ky, 128), BF16),
            pltpu.VMEM((PARTS, nz, 2 * group, kz, 128), BF16),
            pltpu.VMEM((2, PARTS, steps_y, group, ky, 128), BF16),
            pltpu.VMEM((2, PARTS, steps_z, 2 * group, kz, 128), BF16),
            pltpu.VMEM((nx, ky + 2 * kz, 128), BF16),
            pltpu.VMEM((nx, ky + 2 * kz, 128), BF16),
            pltpu.VMEM((nz, ky, 128), BF16),
            pltpu.VMEM((2, kz, 128), BF16),
            pltpu.VMEM((ny, kz, 128), BF16),
            pltpu.VMEM((Y_LO, ky, 128), BF16),
            pltpu.VMEM((nz, kz, 128), BF16),
            dma((3,)),
            dma((PARTS, 2 * group)),
            dma((PARTS + 1, 2 * group)), dma((PARTS + 1, 2 * group)),
            dma(()), dma(()),
            dma((max(Y_LO // 2, 1),)), dma(()),
            dma((2, 2, steps_x, 2)), dma((2, 2, steps_x, 2)),
            dma((nx,)), dma((nx,)),
            pltpu.SemaphoreType.REGULAR((max(nx // 2 - 1, 1),)),
            dma((2, 2, PARTS, max(steps_y, steps_z))), dma((2, 2, PARTS, max(steps_y, steps_z))),
            dma((nx,)), dma((nx,)),
            dma((nz,)), dma((nz,)),
            dma((ny,)), dma((ny,)),
            dma((Y_LO,)), dma((Y_LO,)),
            dma((nz,)), dma((nz,)),
        ],
        compiler_params=pltpu.CompilerParams(
            collective_id=0, has_side_effects=True, vmem_limit_bytes=55_300_000
        ),
    )(tokens, key_weight, key_grad, cosine, sine, gain)
    return (keys, weight_grad, gain_grad.reshape(ROWS))


def solution(mesh):
    return jax.shard_map(
        local,
        mesh=mesh,
        in_specs=(
            P(("wide", "narrow"), None),
            P("narrow"),
            P("narrow", None),
            P(("wide", "narrow"), None),
        ),
        out_specs=(P(("wide", "narrow"), None), P("narrow", None), P("narrow")),
        check_vma=False,
    )
```
